32 devices in a mesh: grp: 2 (over x), tok: 4 (over z), head: 4 (over y, core).
Axes of the slice: x: 2, y: 2, z: 4, core: 2. Of those that a mesh axis runs over, the one named last changes fastest.
Arguments:
- views: bfloat16 [2, 2, 768, 1024], P('grp', None, 'tok'), may hold values from -6 to 6
- q_weight: bfloat16 [1024, 1024], P(None, 'head'), may hold values from -0.1875 to 0.1875
- k_weight: bfloat16 [1024, 1024], P(None, 'head'), may hold values from -0.1875 to 0.1875
- v_weight: bfloat16 [1024, 1024], P(None, 'head'), may hold values from -0.1875 to 0.1875
- rate_weight: bfloat16 [1024, 4], P(None, 'head'), may hold values from -0.1875 to 0.1875
- fast_in: float32 [4, 256, 1024], P('head', None, 'tok'), may hold values from -0.375 to 0.375
- fast_out: float32 [4, 512, 256], P('head', None, 'tok'), may hold values from -0.25 to 0.25
- out_gain: float32 [1024], P('head'), may hold values from 0.1 to 1.9
Outputs:
- rendered: bfloat16 [2, 2, 768, 1024], P('grp', None, 'tok', 'head')
The draws below stay inside these ranges and needn't reach their ends.
All inputs are finite; a program needn't handle non-finite values.
Results may differ from the reference program's by a relative error of at most 0.013.
Values may be sent and summed in bfloat16 or wider, within the bound.
A program may use at most 64 MiB of HBM per device.

```python
import math
import jax
import jax.numpy as jnp
from jax import lax

D = 1024
H = 4
DH = 256
HF = 512
SPANS = 2
TOKENS = 768


def shard_levels(rng, extent, split, smallest, largest):
    factor_of, own = 1.0, jax.random.fold_in(rng, 6)
    for axis_at, blocks in split:
        draws = jnp.exp(jax.random.uniform(jax.random.fold_in(own, axis_at), (blocks,), jnp.float32, smallest / len(split), largest / len(split)))
        factor_of = factor_of * jnp.repeat(draws, extent[axis_at] // blocks).reshape([-1 if axis == axis_at else 1 for axis in range(len(extent))])
    return factor_of


def gaussian(stream_key, dims, deviation, most, cuts=(), dtype=jnp.bfloat16):
    drawn = deviation * jax.random.normal(stream_key, dims, jnp.float32)
    if cuts:
        drawn = drawn * shard_levels(stream_key, dims, cuts, -0.22, 0.18)
    return jnp.clip(drawn, -most, most).astype(dtype)


def setup_inputs(seed: int = 0) -> dict:
    key_list = jax.random.split(jax.random.key(seed), 9)
    return {
        "views": gaussian(key_list[0], (2, SPANS, TOKENS, D), 1.0, 6.0, ((0, 2), (2, 4))),
        "q_weight": gaussian(key_list[1], (D, D), D ** -0.5, 0.1875, ((1, 4),)),
        "k_weight": gaussian(key_list[2], (D, D), D ** -0.5, 0.1875, ((1, 4),)),
        "v_weight": gaussian(key_list[3], (D, D), D ** -0.5, 0.1875, ((1, 4),)),
        "rate_weight": gaussian(key_list[4], (D, H), D ** -0.5, 0.1875, ((1, 4),)),
        "fast_in": gaussian(key_list[5], (H, DH, 2 * HF), DH ** -0.5, 0.375, ((0, 4), (2, 4)), jnp.float32),
        "fast_out": gaussian(key_list[6], (H, HF, DH), HF ** -0.5, 0.25, ((0, 4), (2, 4)), jnp.float32),
        "out_gain": jnp.clip(1.0 + 0.18 * jax.random.normal(key_list[7], (D,), jnp.float32), 0.1, 1.9),
    }


norm_eps = 1e-06
out_eps = 1e-05
step_coef = 0.3
momentum_keep = 0.5

def rms_scale(values):
    return values * lax.rsqrt(lax.optimization_barrier(jnp.mean(values * values, axis=-1, keepdims=True)) + norm_eps)

def contract_rows(left, right):
    return lax.dot_general(left, right, (((0,), (0,)), ((), ())), preferred_element_type=jnp.float32)

def contract_cols(left, right):
    return lax.dot_general(left, right, (((1,), (1,)), ((), ())), preferred_element_type=jnp.float32)

def fast_grads(inputs, key_proj, value_proj, rate_proj, copy_in, copy_out, step_size):
    hidden_units = copy_out.shape[0]
    keyed = rms_scale(jnp.dot(inputs, key_proj, preferred_element_type=jnp.float32)).astype(jnp.bfloat16)
    valued = jnp.dot(inputs, value_proj, preferred_element_type=jnp.float32)
    rates = jax.nn.softplus(jnp.dot(inputs, rate_proj, preferred_element_type=jnp.float32))
    upstream = (-(step_size * rates) * valued).astype(jnp.bfloat16)
    pre_act = jnp.dot(keyed, copy_in, preferred_element_type=jnp.float32)
    gate = pre_act[:, :hidden_units]
    upper = pre_act[:, hidden_units:]
    sigma = jax.nn.sigmoid(gate)
    active = gate * sigma
    hidden = (active * upper).astype(jnp.bfloat16)
    grad_out = contract_rows(hidden, upstream)
    back = contract_cols(upstream, copy_out)
    back_pre = jnp.concatenate([back * upper * sigma * (1.0 + gate * (1.0 - sigma)), back * active], axis=1).astype(jnp.bfloat16)
    grad_in = contract_rows(keyed, back_pre)
    return (grad_in, grad_out)

def fast_apply(queries, copy_in, copy_out):
    hidden_units = copy_out.shape[0]
    pre_act = jnp.dot(queries, copy_in, preferred_element_type=jnp.float32)
    gate = pre_act[:, :hidden_units]
    upper = pre_act[:, hidden_units:]
    hidden = (gate * jax.nn.sigmoid(gate) * upper).astype(jnp.bfloat16)
    return jnp.dot(hidden, copy_out, preferred_element_type=jnp.float32)

def renormalize(trial, base_squares):
    return trial * jnp.sqrt(base_squares) * lax.rsqrt(lax.optimization_barrier(jnp.mean(trial * trial, axis=0, keepdims=True)) + norm_eps)

def reference(views, q_weight, k_weight, v_weight, rate_weight, fast_in, fast_out, out_gain):
    spans = views.shape[1]
    heads = fast_in.shape[0]
    head_size = fast_in.shape[1]
    step_size = step_coef / math.sqrt(views.shape[2])
    state_in = [fast_in[h] for h in range(heads)]
    state_out = [fast_out[h] for h in range(heads)]
    base_in = [lax.optimization_barrier(jnp.mean(fast_in[h] * fast_in[h], axis=0, keepdims=True)) for h in range(heads)]
    base_out = [lax.optimization_barrier(jnp.mean(fast_out[h] * fast_out[h], axis=0, keepdims=True)) for h in range(heads)]
    moment_in = [jnp.zeros_like(fast_in[h]) for h in range(heads)]
    moment_out = [jnp.zeros_like(fast_out[h]) for h in range(heads)]
    copies_in = [state_in[h].astype(jnp.bfloat16) for h in range(heads)]
    copies_out = [state_out[h].astype(jnp.bfloat16) for h in range(heads)]
    groups = [[], []]
    for span in range(spans):
        inputs = views[0, span]
        for h in range(heads):
            cols = slice(h * head_size, (h + 1) * head_size)
            grad_in, grad_out = fast_grads(inputs, k_weight[:, cols], v_weight[:, cols], rate_weight[:, h:h + 1], copies_in[h], copies_out[h], step_size)
            moment_in[h] = momentum_keep * moment_in[h] + grad_in
            moment_out[h] = momentum_keep * moment_out[h] + grad_out
            state_in[h] = renormalize(state_in[h] - moment_in[h], base_in[h])
            state_out[h] = renormalize(state_out[h] - moment_out[h], base_out[h])
            copies_in[h] = state_in[h].astype(jnp.bfloat16)
            copies_out[h] = state_out[h].astype(jnp.bfloat16)
        for group in range(2):
            pieces = []
            for h in range(heads):
                cols = slice(h * head_size, (h + 1) * head_size)
                queries = rms_scale(jnp.dot(views[group, span], q_weight[:, cols], preferred_element_type=jnp.float32)).astype(jnp.bfloat16)
                pieces.append(fast_apply(queries, copies_in[h], copies_out[h]))
            joined = jnp.concatenate(pieces, axis=1)
            normed = joined * lax.rsqrt(lax.optimization_barrier(jnp.mean(joined * joined, axis=1, keepdims=True)) + out_eps) * out_gain
            groups[group].append(normed.astype(jnp.bfloat16))
    return jnp.stack([jnp.stack(groups[0]), jnp.stack(groups[1])])
```

```python
import functools
import math

import jax
import jax.numpy as jnp
from jax import lax
from jax.experimental import pallas as pl
from jax.experimental.pallas import tpu as pltpu
from jax.sharding import PartitionSpec as P

norm_eps = 1e-06
out_eps = 1e-05
step_coef = 0.3
momentum_keep = 0.5


def spread(value, axis, source):
    kept = jnp.where(lax.axis_index(axis) == source, value, 0).astype(value.dtype)
    return lax.psum(kept, axis)


def rms_scale(values):
    return values * lax.rsqrt(jnp.mean(values * values, axis=-1, keepdims=True) + norm_eps)


def contract_rows(left, right):
    return lax.dot_general(
        left, right, (((0,), (0,)), ((), ())), preferred_element_type=jnp.float32
    )


def contract_cols(left, right):
    return lax.dot_general(
        left, right, (((1,), (1,)), ((), ())), preferred_element_type=jnp.float32
    )


def fast_apply(queries, copy_in, copy_out):
    hidden_units = copy_out.shape[0]
    pre_act = jnp.dot(queries, copy_in, preferred_element_type=jnp.float32)
    gate = pre_act[:, :hidden_units]
    upper = pre_act[:, hidden_units:]
    hidden = (gate * jax.nn.sigmoid(gate) * upper).astype(jnp.bfloat16)
    return jnp.dot(hidden, copy_out, preferred_element_type=jnp.float32)


def by_collectives(views, q_weight, k_weight, v_weight, rate_weight, fast_in, fast_out, out_gain):
    tok_count = lax.axis_size("tok")
    is_input = lax.axis_index("grp") == 0
    spans = views.shape[1]
    head_size = fast_in.shape[1]
    hidden_units = fast_out.shape[1]
    step_size = step_coef / math.sqrt(views.shape[2] * tok_count)
    width_all = head_size * lax.axis_size("head")
    whole_in, whole_out = (
        lax.all_gather(fast_in, "tok", axis=2, tiled=True),
        lax.all_gather(fast_out, "tok", axis=2, tiled=True),
    )
    whole_in = whole_in[0]
    whole_out = whole_out[0]
    copy_in = whole_in.astype(jnp.bfloat16)
    copy_out = whole_out.astype(jnp.bfloat16)
    state_in = fast_in[0]
    state_out = fast_out[0]
    base_in = jnp.mean(state_in * state_in, axis=0, keepdims=True)
    base_out = jnp.mean(state_out * state_out, axis=0, keepdims=True)
    moment_in = jnp.zeros_like(state_in)
    moment_out = jnp.zeros_like(state_out)

    def input_grads(inputs, given_in, given_out):
        keyed = rms_scale(jnp.dot(inputs, k_weight, preferred_element_type=jnp.float32)).astype(
            jnp.bfloat16
        )
        valued = jnp.dot(inputs, v_weight, preferred_element_type=jnp.float32)
        rates = jax.nn.softplus(jnp.dot(inputs, rate_weight, preferred_element_type=jnp.float32))
        upstream = (-(step_size * rates) * valued).astype(jnp.bfloat16)
        pre_act = jnp.dot(keyed, given_in, preferred_element_type=jnp.float32)
        gate = pre_act[:, :hidden_units]
        upper = pre_act[:, hidden_units:]
        sigma = jax.nn.sigmoid(gate)
        active = gate * sigma
        hidden = (active * upper).astype(jnp.bfloat16)
        grad_out = contract_rows(hidden, upstream)
        back = contract_cols(upstream, given_out)
        back_pre = jnp.concatenate(
            [back * upper * sigma * (1.0 + gate * (1.0 - sigma)), back * active], axis=1
        ).astype(jnp.bfloat16)
        grad_in = contract_rows(keyed, back_pre)
        return (grad_in, grad_out)

    def novel_grads(inputs, given_in, given_out):
        return (
            jnp.zeros((head_size, 2 * hidden_units), jnp.float32),
            jnp.zeros((hidden_units, head_size), jnp.float32),
        )

    outputs = []
    for span in range(spans):
        inputs = views[0, span]
        queries = rms_scale(jnp.dot(inputs, q_weight, preferred_element_type=jnp.float32)).astype(
            jnp.bfloat16
        )
        grads = lax.cond(is_input, input_grads, novel_grads, inputs, copy_in, copy_out)
        grad_in, grad_out = lax.psum_scatter(grads, "tok", scatter_dimension=1, tiled=True)
        moment_in = momentum_keep * moment_in + grad_in
        moment_out = momentum_keep * moment_out + grad_out
        trial_in = state_in - moment_in
        trial_out = state_out - moment_out
        mean_in = jnp.mean(trial_in * trial_in, axis=0, keepdims=True)
        mean_out = jnp.mean(trial_out * trial_out, axis=0, keepdims=True)
        state_in = trial_in * jnp.sqrt(base_in) * lax.rsqrt(mean_in + norm_eps)
        state_out = trial_out * jnp.sqrt(base_out) * lax.rsqrt(mean_out + norm_eps)
        part_in = state_in.astype(jnp.bfloat16)
        part_out = state_out.astype(jnp.bfloat16)
        copy_in, copy_out = (
            lax.all_gather(part_in, "tok", axis=1, tiled=True),
            lax.all_gather(part_out, "tok", axis=1, tiled=True),
        )
        copy_in, copy_out = (spread(copy_in, "grp", 0), spread(copy_out, "grp", 0))
        produced = fast_apply(queries, copy_in, copy_out)
        squares = lax.psum(jnp.sum(produced * produced, axis=1), "head")
        normed = produced * lax.rsqrt(squares / width_all + out_eps)[:, None] * out_gain
        outputs.append(normed.astype(jnp.bfloat16))
    return jnp.stack(outputs)[None]


def fused_kernel(
    tok_count, grp_count, head_count,
    views_ref, q_hbm, k_hbm, v_hbm, rate_hbm, in_hbm, out_hbm, gain_hbm,
    res_ref,
    local_views, q_ref, k_ref, v_ref, rate_ref, in_ref, out_ref, gain_ref,
    pieces, packed, queries, keys, ups, moment_in, moment_out, state_in, state_out, copy_in, copy_out,
    base_in, base_out, produced, squares,
    load_sem, own_sem,
    z_send, z_recv, x_send, x_recv, y_send, y_recv,
    c1_send, c1_recv, c2_send, c2_recv, wz_send, wz_recv, wx_send, wx_recv, sq_send, sq_recv,
):
    tok, grp, head = lax.axis_index("tok"), lax.axis_index("grp"), lax.axis_index("head")
    spans, rows, width = views_ref.shape[1:]
    piece = pieces.shape[-1]
    head_size, block_in = in_ref.shape
    block_out, hidden_units = out_ref.shape
    fold = packed.shape[-1] - block_in
    folds = hidden_units // fold
    strip = head_size // 4
    strips = [slice(p * strip, (p + 1) * strip) for p in range(4)]
    step_size = step_coef / math.sqrt(rows * tok_count)
    last_tok = tok_count - 1
    far_bit = head_count // 2
    far_head = jnp.where(head < far_bit, head + far_bit, head - far_bit)
    near_head = head + 1 - 2 * lax.rem(head, 2)
    other = {"grp": 1 - grp}
    far = {"head": far_head}
    near = {"head": near_head}
    above = {"tok": jnp.minimum(tok + 1, last_tok)}
    below = {"tok": jnp.maximum(tok - 1, 0)}
    skip = {"tok": jnp.where(tok * 2 < tok_count, tok + 2, tok - 2)}
    outer = {"tok": jnp.where(tok * 2 < tok_count, jnp.maximum(tok - 1, 0), jnp.minimum(tok + 1, last_tok))}
    has_above, has_below = tok < last_tok, tok > 0
    is_input, is_novel = grp == 0, grp == 1

    low = tok * 2 < tok_count
    inner = jnp.where(low, tok, last_tok - tok)
    flip = jnp.where(low, 1, -1)

    def shard(place):
        if place == 0:
            return tok
        step = (place + 1) // 2 * (1 if place % 2 else -1)
        return jnp.where(
            place <= 2 * inner, tok + flip * step, jnp.where(low, place, last_tok - place)
        )

    shards = [shard(i) for i in range(tok_count)]
    sent = []

    def remote(src, dst, send, recv, target):
        return pltpu.make_async_remote_copy(
            src_ref=src, dst_ref=dst, send_sem=send, recv_sem=recv,
            device_id=target, device_id_type=pl.DeviceIdType.MESH,
        )

    def same(ref, send, recv, target):
        return remote(ref, ref, send, recv, target)

    def send(copy, cond=None):
        sent.append((copy, cond))
        if cond is None:
            copy.start()
        else:
            pl.when(cond)(copy.start)

    def view_piece(span, h, part):
        start = pl.multiple_of((h * grp_count + part) * piece, piece)
        return views_ref.at[0, span, :, pl.ds(start, piece)]

    def block(span, i, h, part):
        return pieces.at[span, shards[i], h, part]

    loads = [
        pltpu.make_async_copy(src, dst, load_sem.at[n])
        for n, (src, dst) in enumerate([
            (in_hbm.at[0], in_ref), (out_hbm.at[0], out_ref), (views_ref.at[0], local_views), (q_hbm, q_ref),
            (k_hbm, k_ref), (v_hbm, v_ref), (rate_hbm, rate_ref), (gain_hbm, gain_ref),
        ])
    ]
    own = [
        [
            pltpu.make_async_copy(view_piece(s, h, g), pieces.at[s, tok, h, g], own_sem.at[s, h, g])
            for h in range(head_count) for g in range(grp_count)
        ]
        for s in range(spans)
    ]

    barrier = pltpu.get_barrier_semaphore()

    def greet(target):
        pl.semaphore_signal(barrier, inc=1, device_id=target, device_id_type=pl.DeviceIdType.MESH)

    greet(other)
    greet(skip)
    greet(far)
    greet(near)
    pl.when(has_above)(lambda: greet(above))
    pl.when(has_below)(lambda: greet(below))
    for copy in loads:
        copy.start()

    @pl.when(is_input)
    def _():
        for copies in own:
            for copy in copies:
                copy.start()

    loads[0].wait()
    loads[1].wait()
    packed[tok, :, :block_in] = in_ref[...].astype(jnp.bfloat16)
    for f in range(folds):
        packed[tok, f * block_out:(f + 1) * block_out, block_in:] = out_ref[
            :, f * fold:(f + 1) * fold
        ].astype(jnp.bfloat16)
    pl.semaphore_wait(barrier, 4 + jnp.where(has_above, 1, 0) + jnp.where(has_below, 1, 0))

    parts = range(grp_count)
    quarters = range(len(strips))
    relays = has_above & has_below
    sides = (is_input, is_novel)

    def carrier(s, part):
        return ((0, 0), (0, 1))[s][part]

    def weight_carrier(q):
        return (0, 1, 1, 1)[q]

    def z_copy(s, i, part, way, target, fresh=False):
        src = view_piece(s, head, part) if fresh else block(s, i, head, part)
        return remote(
            src, block(s, i, head, part), z_send.at[s, i, part, way], z_recv.at[s, shards[i], part], target
        )

    def w_copy(i, q, way, target):
        return same(packed.at[shards[i], strips[q]], wz_send.at[i, q, way], wz_recv.at[shards[i], q], target)

    def x_copy(s, i, part, fresh=False):
        src = view_piece(s, head, part) if fresh else block(s, i, head, part)
        return remote(src, block(s, i, head, part), x_send.at[s, i, part], x_recv.at[s, i, part], other)

    def y_copy(s, i, part):
        return same(block(s, i, head, part), y_send.at[s, i, part], y_recv.at[s, i, part], far)

    def c_copy(s, i, n, part):
        h, snd, rcv = ((head, c1_send, c1_recv), (far_head, c2_send, c2_recv))[n]
        return same(block(s, i, h, part), snd.at[s, i, part], rcv.at[s, i, part], near)

    def x_weights(i, q):
        return same(packed.at[shards[i], strips[q]], wx_send.at[i, q], wx_recv.at[i, q], other)

    def fan(side, copy):
        for way, (target, cond) in enumerate(((above, has_above), (below, has_below), (skip, None))):
            send(copy(way, target), side if cond is None else cond & side)

    def own_views(s, part):
        fresh = carrier(s, part) == 0
        fan(sides[carrier(s, part)], lambda way, target: z_copy(s, 0, part, way, target, fresh))

    def own_weights(q):
        fan(sides[weight_carrier(q)], lambda way, target: w_copy(0, q, way, target))

    def own_across(s, part):
        send(x_copy(s, 0, part, True), is_input)

    def spread_on(s, i, part, cond):
        send(y_copy(s, i, part), cond)
        send(c_copy(s, i, 0, part), cond)

    def start_own(s, part):
        if carrier(s, part) == 0:
            own_views(s, part)

    def pass_z(s, i, part):
        side = sides[carrier(s, part)]
        pl.when(side)(z_copy(s, i, part, 0, above).wait_recv)
        if i == last_tok:
            send(z_copy(s, i, part, 0, outer), relays & side)
        send(x_copy(s, i, part), side)
        spread_on(s, i, part, side)

    def pass_x(s, i, part):
        side = is_novel if i == 0 else sides[1 - carrier(s, part)]
        pl.when(side)(x_copy(s, i, part).wait_recv)
        if i == 0 and carrier(s, part) == 1:
            own_views(s, part)
        spread_on(s, i, part, side)

    def pass_y(s, i, part):
        cond = is_novel if i == 0 else None
        if cond is None:
            y_copy(s, i, part).wait_recv()
        else:
            pl.when(cond)(y_copy(s, i, part).wait_recv)
        send(c_copy(s, i, 1, part), cond)

    def take(s, i):
        def waits():
            for n in range(2):
                for part in parts:
                    c_copy(s, i, n, part).wait_recv()
        if i == 0:
            pl.when(is_novel)(waits)

            @pl.when(is_input)
            def _():
                for copy in own[s]:
                    copy.wait()
        else:
            waits()
        project(s, i)

    def pass_weights(i, q):
        side = sides[weight_carrier(q)]
        pl.when(side)(w_copy(i, q, 0, above).wait_recv)
        if i == last_tok:
            send(w_copy(i, q, 0, outer), relays & side)
        send(x_weights(i, q), side)

    def unpack_all():
        for i in range(1, tok_count):
            for q in quarters:
                pl.when(sides[1 - weight_carrier(q)])(x_weights(i, q).wait_recv)
        for t in range(tok_count):
            unpack(t)
        base_out[...] = jnp.sqrt(jnp.mean(state_out[...] * state_out[...], axis=1, keepdims=True))
        moment_in[...] = jnp.zeros_like(moment_in)
        moment_out[...] = jnp.zeros_like(moment_out)

    def project_queries(span):
        queries[span] = rms_scale(
            jnp.dot(local_views[span], q_ref[...], preferred_element_type=jnp.float32)
        ).astype(jnp.bfloat16)

    def project(span, i):
        t = shards[i]
        inputs = jnp.concatenate(
            [pieces[span, t, h, g] for h in range(head_count) for g in range(grp_count)], axis=1
        )
        keys[span, i] = rms_scale(
            jnp.dot(inputs, k_ref[...], preferred_element_type=jnp.float32)
        ).astype(jnp.bfloat16)
        valued = jnp.dot(inputs, v_ref[...], preferred_element_type=jnp.float32)
        raw = contract_cols(inputs, jnp.broadcast_to(rate_ref[...], (8, width)))[:, :1]
        rates = jnp.maximum(raw, 0.0) + jnp.log1p(jnp.exp(-jnp.abs(raw)))
        ups[span, i] = (-(step_size * rates) * valued).astype(jnp.bfloat16)

    def unpack(t):
        cols = slice(t * block_in, (t + 1) * block_in)
        given = packed[t, :, :block_in]
        wide = given.astype(jnp.float32)
        copy_in[:, cols] = given
        state_in[:, cols] = wide
        base_in[:, cols] = jnp.sqrt(jnp.mean(wide * wide, axis=0, keepdims=True))
        for f in range(folds):
            part = slice(f * fold, (f + 1) * fold)
            turned = slice(t * block_out, (t + 1) * block_out)
            given = packed[t, f * block_out:(f + 1) * block_out, block_in:]
            copy_out[turned, part] = given
            state_out[turned, part] = given.astype(jnp.float32)

    def add_grads(span, t):
        keyed, upstream = keys[span, t], ups[span, t]
        gate = jnp.dot(keyed, copy_in[:, :hidden_units], preferred_element_type=jnp.float32)
        upper = jnp.dot(keyed, copy_in[:, hidden_units:], preferred_element_type=jnp.float32)
        sigma = jax.nn.sigmoid(gate)
        active = gate * sigma
        hidden = (active * upper).astype(jnp.bfloat16)
        moment_out[...] += contract_rows(upstream, hidden)
        back = jnp.dot(upstream, copy_out[...], preferred_element_type=jnp.float32)
        back_gate = (back * upper * sigma * (1.0 + gate * (1.0 - sigma))).astype(jnp.bfloat16)
        back_upper = (back * active).astype(jnp.bfloat16)
        moment_in[:, :hidden_units] += contract_rows(keyed, back_gate)
        moment_in[:, hidden_units:] += contract_rows(keyed, back_upper)

    def renormalize(state, moment, base, axis):
        trial = state - moment
        mean = jnp.mean(trial * trial, axis=axis, keepdims=True)
        return trial * base * lax.rsqrt(mean + norm_eps)

    def update(s):
        for t in range(tok_count):
            cols = slice(t * block_in, (t + 1) * block_in)
            fresh = renormalize(state_in[:, cols], moment_in[:, cols], base_in[:, cols], 0)
            copy_in[:, cols] = fresh.astype(jnp.bfloat16)
            if s + 1 < spans:
                state_in[:, cols] = fresh
                moment_in[:, cols] *= momentum_keep
            turned = slice(t * block_out, (t + 1) * block_out)
            fresh = renormalize(state_out[turned], moment_out[turned], base_out[turned], 1)
            copy_out[turned] = fresh.astype(jnp.bfloat16)
            if s + 1 < spans:
                state_out[turned] = fresh
                moment_out[turned] *= momentum_keep

    square = [
        [
            same(squares.at[s, head], sq_send.at[s, d], sq_recv.at[s, d],
                 {"head": lax.rem(head + d + 1, head_count)})
            for d in range(head_count - 1)
        ]
        for s in range(spans)
    ]

    def apply(s):
        pre_act = jnp.dot(queries[s], copy_in[...], preferred_element_type=jnp.float32)
        gate = pre_act[:, :hidden_units]
        hidden = (gate * jax.nn.sigmoid(gate) * pre_act[:, hidden_units:]).astype(jnp.bfloat16)
        made = contract_cols(hidden, copy_out[...])
        produced[s] = made
        sums = jnp.sum(made * made, axis=1, keepdims=True)
        squares[s, head] = jnp.transpose(jnp.broadcast_to(sums, (rows, 128)))[:8]
        for copy in square[s]:
            send(copy)

    def finish(s):
        for copy in square[s]:
            copy.wait_recv()
        total = squares[s, 0]
        for h in range(1, head_count):
            total = total + squares[s, h]
        scale = lax.rsqrt(total / (head_size * head_count) + out_eps)
        column = jnp.transpose(jnp.concatenate([scale] * 16, axis=0))[:, :1]
        res_ref[0, s] = (produced[s] * column * gain_ref[...]).astype(jnp.bfloat16)

    own_across(1, 1)
    start_own(0, 0)
    own_across(0, 1)
    own_weights(1)
    pass_x(1, 0, 1)
    pass_x(0, 0, 1)
    own_across(0, 0)
    pass_x(0, 0, 0)
    pass_x(1, 0, 0)
    own_across(1, 0)
    start_own(0, 1)
    pass_z(0, 2, 0)
    pass_weights(1, 1)
    pass_z(0, 1, 0)
    pass_z(0, 1, 1)
    own_weights(3)
    pass_weights(1, 3)
    for copy in loads[2:]:
        copy.wait()
    project_queries(0)
    own_weights(2)
    pass_z(1, 2, 1)
    start_own(1, 0)
    pass_z(0, 2, 1)
    pass_weights(2, 1)
    pass_x(0, 1, 0)
    pass_x(0, 1, 1)
    pass_z(0, 3, 0)
    pass_x(0, 2, 0)
    pass_z(1, 1, 0)
    own_weights(0)
    pass_z(1, 2, 0)
    pass_weights(2, 3)
    pass_x(0, 2, 1)
    pass_z(1, 1, 1)
    pass_weights(3, 1)
    pass_z(0, 3, 1)
    pass_z(1, 3, 0)
    pass_weights(2, 2)
    pass_x(1, 2, 1)
    pass_x(0, 3, 0)
    pass_y(0, 1, 0)
    project_queries(1)
    pass_weights(3, 3)
    pass_x(0, 3, 1)
    pass_weights(2, 0)
    pass_weights(1, 2)
    pass_y(0, 0, 1)
    pass_y(0, 0, 0)
    pass_weights(1, 0)
    pass_weights(3, 0)
    pass_weights(3, 2)
    pass_y(1, 0, 1)
    pass_y(0, 2, 1)
    pass_x(1, 1, 0)
    take(0, 0)
    pass_y(0, 1, 1)
    pass_x(1, 2, 0)
    pass_z(1, 3, 1)
    pass_x(1, 3, 0)
    pass_y(1, 0, 0)
    pass_x(1, 1, 1)
    pass_y(0, 2, 0)
    pass_y(0, 3, 1)
    take(0, 1)
    pass_y(1, 2, 1)
    take(1, 0)
    pass_y(0, 3, 0)
    take(0, 2)
    unpack_all()
    add_grads(0, 0)
    pass_y(1, 1, 0)
    pass_y(1, 2, 0)
    take(0, 3)
    pass_y(1, 1, 1)
    pass_x(1, 3, 1)
    add_grads(0, 1)
    add_grads(0, 3)
    add_grads(0, 2)
    update(0)
    start_own(1, 1)
    take(1, 1)
    take(1, 2)
    apply(0)
    pass_y(1, 3, 0)
    pass_y(1, 3, 1)
    add_grads(1, 2)
    add_grads(1, 1)
    add_grads(1, 0)
    take(1, 3)
    add_grads(1, 3)
    update(1)
    apply(1)
    finish(0)
    finish(1)
    for copy, cond in sent:
        if cond is None:
            copy.wait_send()
        else:
            pl.when(cond)(copy.wait_send)


def by_kernel(sizes, views, q_weight, k_weight, v_weight, rate_weight, fast_in, fast_out, out_gain):
    tok_count, grp_count, head_count = sizes
    _, spans, rows, width = views.shape
    _, head_size, block_in = fast_in.shape
    _, hidden_units, block_out = fast_out.shape
    piece = width // (grp_count * head_count)
    fold = hidden_units * block_out // head_size
    dma = pltpu.SemaphoreType.DMA
    vmem = pltpu.VMEM
    return pl.pallas_call(
        functools.partial(fused_kernel, tok_count, grp_count, head_count),
        out_shape=jax.ShapeDtypeStruct((1, spans, rows, head_size), jnp.bfloat16),
        in_specs=[pl.BlockSpec(memory_space=pl.ANY)] * 8,
        out_specs=pl.BlockSpec(memory_space=pltpu.VMEM),
        scratch_shapes=[
            vmem((spans, rows, width), jnp.bfloat16),
            *[vmem((width, head_size), jnp.bfloat16)] * 3,
            vmem((1, width), jnp.bfloat16),
            vmem((head_size, block_in), jnp.float32),
            vmem((block_out, hidden_units), jnp.float32),
            vmem((1, head_size), jnp.float32),
            vmem((spans, tok_count, head_count, grp_count, rows, piece), jnp.bfloat16),
            vmem((tok_count, head_size, block_in + fold), jnp.bfloat16),
            vmem((spans, rows, head_size), jnp.bfloat16),
            vmem((spans, tok_count, rows, head_size), jnp.bfloat16),
            vmem((spans, tok_count, rows, head_size), jnp.bfloat16),
            vmem((head_size, 2 * hidden_units), jnp.float32),
            vmem((head_size, hidden_units), jnp.float32),
            vmem((head_size, 2 * hidden_units), jnp.float32),
            vmem((head_size, hidden_units), jnp.float32),
            vmem((head_size, 2 * hidden_units), jnp.bfloat16),
            vmem((head_size, hidden_units), jnp.bfloat16),
            vmem((1, 2 * hidden_units), jnp.float32),
            vmem((head_size, 1), jnp.float32),
            vmem((spans, rows, head_size), jnp.float32),
            vmem((spans, head_count, 8, rows), jnp.float32),
            dma((8,)), dma((spans, head_count, grp_count)),
            dma((spans, tok_count, grp_count, 3)), dma((spans, tok_count, grp_count)),
            *[dma((spans, tok_count, grp_count))] * 8,
            dma((tok_count, 4, 3)), dma((tok_count, 4)),
            *[dma((tok_count, 4))] * 2,
            *[dma((spans, head_count - 1))] * 2,
        ],
        compiler_params=pltpu.CompilerParams(collective_id=0, has_side_effects=True),
        name="fused_layer",
    )(
        views, q_weight, k_weight, v_weight, rate_weight.T, fast_in,
        jnp.swapaxes(fast_out, 1, 2), out_gain.reshape(1, -1),
    )


def local(sizes, views, *rest):
    tok_count, grp_count, head_count = sizes
    fast_in, fast_out = rest[4], rest[5]
    head_size, hidden_units = fast_in.shape[1], fast_out.shape[1]
    piece = views.shape[3] // (grp_count * head_count)
    few = tok_count * views.shape[2] <= 4 * head_size
    fits = (
        tok_count == 4 and grp_count == 2 and head_count == 4 and piece % 128 == 0
        and fast_in.shape[2] % 128 == 0 and views.shape[2] % 16 == 0 and head_size % fast_out.shape[2] == 0
        and fast_out.shape[2] * hidden_units % (128 * head_size) == 0 and fast_out.shape[2] % 16 == 0
    )
    if few and fits:
        return by_kernel(sizes, views, *rest)
    return by_collectives(views, *rest)


def solution(mesh):
    sizes = (mesh.shape["tok"], mesh.shape["grp"], mesh.shape["head"])
    placed = (
        P("grp", None, "tok", None),
        P(None, "head"),
        P(None, "head"),
        P(None, "head"),
        P(None, "head"),
        P("head", None, "tok"),
        P("head", None, "tok"),
        P("head"),
    )
    return jax.shard_map(
        functools.partial(local, sizes), mesh=mesh, in_specs=placed, out_specs=P("grp", None, "tok", "head"), check_vma=False
    )
```

```python
import functools
import math

import jax
import jax.numpy as jnp
from jax import lax
from jax.experimental import pallas as pl
from jax.experimental.pallas import tpu as pltpu
from jax.sharding import PartitionSpec as P

norm_eps = 1e-06
out_eps = 1e-05
step_coef = 0.3
momentum_keep = 0.5


def spread(value, axis, source):
    kept = jnp.where(lax.axis_index(axis) == source, value, 0).astype(value.dtype)
    return lax.psum(kept, axis)


def rms_scale(values):
    return values * lax.rsqrt(jnp.mean(values * values, axis=-1, keepdims=True) + norm_eps)


def contract_rows(left, right):
    return lax.dot_general(
        left, right, (((0,), (0,)), ((), ())), preferred_element_type=jnp.float32
    )


def contract_cols(left, right):
    return lax.dot_general(
        left, right, (((1,), (1,)), ((), ())), preferred_element_type=jnp.float32
    )


def fast_apply(queries, copy_in, copy_out):
    hidden_units = copy_out.shape[0]
    pre_act = jnp.dot(queries, copy_in, preferred_element_type=jnp.float32)
    gate = pre_act[:, :hidden_units]
    upper = pre_act[:, hidden_units:]
    hidden = (gate * jax.nn.sigmoid(gate) * upper).astype(jnp.bfloat16)
    return jnp.dot(hidden, copy_out, preferred_element_type=jnp.float32)


def by_collectives(views, q_weight, k_weight, v_weight, rate_weight, fast_in, fast_out, out_gain):
    tok_count = lax.axis_size("tok")
    is_input = lax.axis_index("grp") == 0
    spans = views.shape[1]
    head_size = fast_in.shape[1]
    hidden_units = fast_out.shape[1]
    step_size = step_coef / math.sqrt(views.shape[2] * tok_count)
    width_all = head_size * lax.axis_size("head")
    whole_in, whole_out = (
        lax.all_gather(fast_in, "tok", axis=2, tiled=True),
        lax.all_gather(fast_out, "tok", axis=2, tiled=True),
    )
    whole_in = whole_in[0]
    whole_out = whole_out[0]
    copy_in = whole_in.astype(jnp.bfloat16)
    copy_out = whole_out.astype(jnp.bfloat16)
    state_in = fast_in[0]
    state_out = fast_out[0]
    base_in = jnp.mean(state_in * state_in, axis=0, keepdims=True)
    base_out = jnp.mean(state_out * state_out, axis=0, keepdims=True)
    moment_in = jnp.zeros_like(state_in)
    moment_out = jnp.zeros_like(state_out)

    def input_grads(inputs, given_in, given_out):
        keyed = rms_scale(jnp.dot(inputs, k_weight, preferred_element_type=jnp.float32)).astype(
            jnp.bfloat16
        )
        valued = jnp.dot(inputs, v_weight, preferred_element_type=jnp.float32)
        rates = jax.nn.softplus(jnp.dot(inputs, rate_weight, preferred_element_type=jnp.float32))
        upstream = (-(step_size * rates) * valued).astype(jnp.bfloat16)
        pre_act = jnp.dot(keyed, given_in, preferred_element_type=jnp.float32)
        gate = pre_act[:, :hidden_units]
        upper = pre_act[:, hidden_units:]
        sigma = jax.nn.sigmoid(gate)
        active = gate * sigma
        hidden = (active * upper).astype(jnp.bfloat16)
        grad_out = contract_rows(hidden, upstream)
        back = contract_cols(upstream, given_out)
        back_pre = jnp.concatenate(
            [back * upper * sigma * (1.0 + gate * (1.0 - sigma)), back * active], axis=1
        ).astype(jnp.bfloat16)
        grad_in = contract_rows(keyed, back_pre)
        return (grad_in, grad_out)

    def novel_grads(inputs, given_in, given_out):
        return (
            jnp.zeros((head_size, 2 * hidden_units), jnp.float32),
            jnp.zeros((hidden_units, head_size), jnp.float32),
        )

    outputs = []
    for span in range(spans):
        inputs = views[0, span]
        queries = rms_scale(jnp.dot(inputs, q_weight, preferred_element_type=jnp.float32)).astype(
            jnp.bfloat16
        )
        grads = lax.cond(is_input, input_grads, novel_grads, inputs, copy_in, copy_out)
        grad_in, grad_out = lax.psum_scatter(grads, "tok", scatter_dimension=1, tiled=True)
        moment_in = momentum_keep * moment_in + grad_in
        moment_out = momentum_keep * moment_out + grad_out
        trial_in = state_in - moment_in
        trial_out = state_out - moment_out
        mean_in = jnp.mean(trial_in * trial_in, axis=0, keepdims=True)
        mean_out = jnp.mean(trial_out * trial_out, axis=0, keepdims=True)
        state_in = trial_in * jnp.sqrt(base_in) * lax.rsqrt(mean_in + norm_eps)
        state_out = trial_out * jnp.sqrt(base_out) * lax.rsqrt(mean_out + norm_eps)
        part_in = state_in.astype(jnp.bfloat16)
        part_out = state_out.astype(jnp.bfloat16)
        copy_in, copy_out = (
            lax.all_gather(part_in, "tok", axis=1, tiled=True),
            lax.all_gather(part_out, "tok", axis=1, tiled=True),
        )
        copy_in, copy_out = (spread(copy_in, "grp", 0), spread(copy_out, "grp", 0))
        produced = fast_apply(queries, copy_in, copy_out)
        squares = lax.psum(jnp.sum(produced * produced, axis=1), "head")
        normed = produced * lax.rsqrt(squares / width_all + out_eps)[:, None] * out_gain
        outputs.append(normed.astype(jnp.bfloat16))
    return jnp.stack(outputs)[None]


def fused_kernel(
    tok_count, grp_count, head_count,
    views_ref, q_hbm, k_hbm, v_hbm, rate_hbm, in_hbm, out_hbm, gain_hbm,
    res_ref,
    local_views, q_ref, k_ref, v_ref, rate_ref, in_ref, out_ref, gain_ref,
    pieces, packed, queries, keys, ups, moment_in, moment_out, state_in, state_out, copy_in, copy_out,
    base_in, base_out, produced, squares,
    load_sem, own_sem,
    z_send, z_recv, x_send, x_recv, y_send, y_recv,
    c1_send, c1_recv, c2_send, c2_recv, wz_send, wz_recv, wx_send, wx_recv, sq_send, sq_recv,
):
    tok, grp, head = lax.axis_index("tok"), lax.axis_index("grp"), lax.axis_index("head")
    spans, rows, width = views_ref.shape[1:]
    piece = pieces.shape[-1]
    head_size, block_in = in_ref.shape
    block_out, hidden_units = out_ref.shape
    fold = packed.shape[-1] - block_in
    folds = hidden_units // fold
    strip = head_size // 4
    strips = [slice(p * strip, (p + 1) * strip) for p in range(4)]
    step_size = step_coef / math.sqrt(rows * tok_count)
    last_tok = tok_count - 1
    far_bit = head_count // 2
    far_head = jnp.where(head < far_bit, head + far_bit, head - far_bit)
    near_head = head + 1 - 2 * lax.rem(head, 2)
    other = {"grp": 1 - grp}
    far = {"head": far_head}
    near = {"head": near_head}
    above = {"tok": jnp.minimum(tok + 1, last_tok)}
    below = {"tok": jnp.maximum(tok - 1, 0)}
    skip = {"tok": jnp.where(tok * 2 < tok_count, tok + 2, tok - 2)}
    outer = {"tok": jnp.where(tok * 2 < tok_count, jnp.maximum(tok - 1, 0), jnp.minimum(tok + 1, last_tok))}
    has_above, has_below = tok < last_tok, tok > 0
    is_input, is_novel = grp == 0, grp == 1

    low = tok * 2 < tok_count
    inner = jnp.where(low, tok, last_tok - tok)
    flip = jnp.where(low, 1, -1)

    def shard(place):
        if place == 0:
            return tok
        step = (place + 1) // 2 * (1 if place % 2 else -1)
        return jnp.where(
            place <= 2 * inner, tok + flip * step, jnp.where(low, place, last_tok - place)
        )

    shards = [shard(i) for i in range(tok_count)]
    sent = []

    def remote(src, dst, send, recv, target):
        return pltpu.make_async_remote_copy(
            src_ref=src, dst_ref=dst, send_sem=send, recv_sem=recv,
            device_id=target, device_id_type=pl.DeviceIdType.MESH,
        )

    def same(ref, send, recv, target):
        return remote(ref, ref, send, recv, target)

    def send(copy, cond=None):
        sent.append((copy, cond))
        if cond is None:
            copy.start()
        else:
            pl.when(cond)(copy.start)

    def view_piece(span, h, part):
        start = pl.multiple_of((h * grp_count + part) * piece, piece)
        return views_ref.at[0, span, :, pl.ds(start, piece)]

    def block(span, i, h, part):
        return pieces.at[span, shards[i], h, part]

    loads = [
        pltpu.make_async_copy(src, dst, load_sem.at[n])
        for n, (src, dst) in enumerate([
            (in_hbm.at[0], in_ref), (out_hbm.at[0], out_ref), (views_ref.at[0], local_views), (q_hbm, q_ref),
            (k_hbm, k_ref), (v_hbm, v_ref), (rate_hbm, rate_ref), (gain_hbm, gain_ref),
        ])
    ]
    own = [
        [
            pltpu.make_async_copy(view_piece(s, h, g), pieces.at[s, tok, h, g], own_sem.at[s, h, g])
            for h in range(head_count) for g in range(grp_count)
        ]
        for s in range(spans)
    ]

    barrier = pltpu.get_barrier_semaphore()

    def greet(target):
        pl.semaphore_signal(barrier, inc=1, device_id=target, device_id_type=pl.DeviceIdType.MESH)

    greet(other)
    greet(skip)
    greet(far)
    greet(near)
    pl.when(has_above)(lambda: greet(above))
    pl.when(has_below)(lambda: greet(below))
    for copy in loads:
        copy.start()

    @pl.when(is_input)
    def _():
        for copies in own:
            for copy in copies:
                copy.start()

    loads[0].wait()
    loads[1].wait()
    packed[tok, :, :block_in] = in_ref[...].astype(jnp.bfloat16)
    for f in range(folds):
        packed[tok, f * block_out:(f + 1) * block_out, block_in:] = out_ref[
            :, f * fold:(f + 1) * fold
        ].astype(jnp.bfloat16)
    pl.semaphore_wait(barrier, 4 + jnp.where(has_above, 1, 0) + jnp.where(has_below, 1, 0))

    parts = range(grp_count)
    quarters = range(len(strips))
    relays = has_above & has_below
    sides = (is_input, is_novel)

    def carrier(s, part):
        return ((0, 0), (0, 1))[s][part]

    def weight_carrier(q):
        return (0, 1, 1, 1)[q]

    def z_copy(s, i, part, way, target, fresh=False):
        src = view_piece(s, head, part) if fresh else block(s, i, head, part)
        return remote(
            src, block(s, i, head, part), z_send.at[s, i, part, way], z_recv.at[s, shards[i], part], target
        )

    def w_copy(i, q, way, target):
        return same(packed.at[shards[i], strips[q]], wz_send.at[i, q, way], wz_recv.at[shards[i], q], target)

    def x_copy(s, i, part, fresh=False):
        src = view_piece(s, head, part) if fresh else block(s, i, head, part)
        return remote(src, block(s, i, head, part), x_send.at[s, i, part], x_recv.at[s, i, part], other)

    def y_copy(s, i, part):
        return same(block(s, i, head, part), y_send.at[s, i, part], y_recv.at[s, i, part], far)

    def c_copy(s, i, n, part):
        h, snd, rcv = ((head, c1_send, c1_recv), (far_head, c2_send, c2_recv))[n]
        return same(block(s, i, h, part), snd.at[s, i, part], rcv.at[s, i, part], near)

    def x_weights(i, q):
        return same(packed.at[shards[i], strips[q]], wx_send.at[i, q], wx_recv.at[i, q], other)

    def fan(side, copy):
        for way, (target, cond) in enumerate(((above, has_above), (below, has_below), (skip, None))):
            send(copy(way, target), side if cond is None else cond & side)

    def own_views(s, part):
        fresh = carrier(s, part) == 0
        fan(sides[carrier(s, part)], lambda way, target: z_copy(s, 0, part, way, target, fresh))

    def own_weights(q):
        fan(sides[weight_carrier(q)], lambda way, target: w_copy(0, q, way, target))

    def own_across(s, part):
        send(x_copy(s, 0, part, True), is_input)

    def spread_on(s, i, part, cond):
        send(y_copy(s, i, part), cond)
        send(c_copy(s, i, 0, part), cond)

    def start_own(s, part):
        if carrier(s, part) == 0:
            own_views(s, part)

    def pass_z(s, i, part):
        side = sides[carrier(s, part)]
        pl.when(side)(z_copy(s, i, part, 0, above).wait_recv)
        if i == last_tok:
            send(z_copy(s, i, part, 0, outer), relays & side)
        send(x_copy(s, i, part), side)
        spread_on(s, i, part, side)

    def pass_x(s, i, part):
        side = is_novel if i == 0 else sides[1 - carrier(s, part)]
        pl.when(side)(x_copy(s, i, part).wait_recv)
        if i == 0 and carrier(s, part) == 1:
            own_views(s, part)
        spread_on(s, i, part, side)

    def pass_y(s, i, part):
        cond = is_novel if i == 0 else None
        if cond is None:
            y_copy(s, i, part).wait_recv()
        else:
            pl.when(cond)(y_copy(s, i, part).wait_recv)
        send(c_copy(s, i, 1, part), cond)

    def take(s, i):
        def waits():
            for n in range(2):
                for part in parts:
                    c_copy(s, i, n, part).wait_recv()
        if i == 0:
            pl.when(is_novel)(waits)

            @pl.when(is_input)
            def _():
                for copy in own[s]:
                    copy.wait()
        else:
            waits()
        project(s, i)

    def pass_weights(i, q):
        side = sides[weight_carrier(q)]
        pl.when(side)(w_copy(i, q, 0, above).wait_recv)
        if i == last_tok:
            send(w_copy(i, q, 0, outer), relays & side)
        send(x_weights(i, q), side)

    def unpack_all():
        for i in range(1, tok_count):
            for q in quarters:
                pl.when(sides[1 - weight_carrier(q)])(x_weights(i, q).wait_recv)
            unpack(shards[i])
        base_out[...] = jnp.sqrt(jnp.mean(state_out[...] * state_out[...], axis=1, keepdims=True))

    def project_queries(span):
        queries[span] = rms_scale(
            jnp.dot(local_views[span], q_ref[...], preferred_element_type=jnp.float32)
        ).astype(jnp.bfloat16)

    def project(span, i):
        t = shards[i]
        inputs = jnp.concatenate(
            [pieces[span, t, h, g] for h in range(head_count) for g in range(grp_count)], axis=1
        )
        lines = slice(i * rows, (i + 1) * rows)
        keys[span, lines] = rms_scale(
            jnp.dot(inputs, k_ref[...], preferred_element_type=jnp.float32)
        ).astype(jnp.bfloat16)
        valued = jnp.dot(inputs, v_ref[...], preferred_element_type=jnp.float32)
        raw = contract_cols(inputs, jnp.broadcast_to(rate_ref[...], (8, width)))[:, :1]
        rates = jnp.maximum(raw, 0.0) + jnp.log1p(jnp.exp(-jnp.abs(raw)))
        ups[span, lines] = (-(step_size * rates) * valued).astype(jnp.bfloat16)

    def unpack(t):
        cols = pl.ds(pl.multiple_of(t * block_in, block_in), block_in)
        given = packed[t, :, :block_in]
        wide = given.astype(jnp.float32)
        copy_in[:, cols] = given
        state_in[:, cols] = wide
        base_in[:, cols] = jnp.sqrt(jnp.mean(wide * wide, axis=0, keepdims=True))
        for f in range(folds):
            part = slice(f * fold, (f + 1) * fold)
            turned = pl.ds(pl.multiple_of(t * block_out, block_out), block_out)
            given = packed[t, f * block_out:(f + 1) * block_out, block_in:]
            copy_out[turned, part] = given
            state_out[turned, part] = given.astype(jnp.float32)

    def add_grads(span, start, count):
        lines = slice(start * rows, (start + count) * rows)
        keyed, upstream = keys[span, lines], ups[span, lines]

        def gather(moment, cols, left, right):
            grads = contract_rows(left, right)
            if span == 0 and start == 0:
                moment[:, cols] = grads
            elif start == 0:
                moment[:, cols] = momentum_keep * moment[:, cols] + grads
            else:
                moment[:, cols] += grads

        first, second = slice(0, hidden_units), slice(hidden_units, 2 * hidden_units)
        gate = jnp.dot(keyed, copy_in[:, first], preferred_element_type=jnp.float32)
        upper = jnp.dot(keyed, copy_in[:, second], preferred_element_type=jnp.float32)
        sigma = jax.nn.sigmoid(gate)
        active = gate * sigma
        hidden = (active * upper).astype(jnp.bfloat16)
        gather(moment_out, first, upstream, hidden)
        back = jnp.dot(upstream, copy_out[...], preferred_element_type=jnp.float32)
        back_gate = (back * upper * sigma * (1.0 + gate * (1.0 - sigma))).astype(jnp.bfloat16)
        back_upper = (back * active).astype(jnp.bfloat16)
        gather(moment_in, first, keyed, back_gate)
        gather(moment_in, second, keyed, back_upper)

    def renormalize(state, moment, base, axis):
        trial = state - moment
        mean = jnp.mean(trial * trial, axis=axis, keepdims=True)
        return trial * base * lax.rsqrt(mean + norm_eps)

    def update(s):
        for t in range(tok_count):
            cols = slice(t * block_in, (t + 1) * block_in)
            fresh = renormalize(state_in[:, cols], moment_in[:, cols], base_in[:, cols], 0)
            copy_in[:, cols] = fresh.astype(jnp.bfloat16)
            if s + 1 < spans:
                state_in[:, cols] = fresh
            turned = slice(t * block_out, (t + 1) * block_out)
            fresh = renormalize(state_out[turned], moment_out[turned], base_out[turned], 1)
            copy_out[turned] = fresh.astype(jnp.bfloat16)
            if s + 1 < spans:
                state_out[turned] = fresh

    square = [
        [
            same(squares.at[s, head], sq_send.at[s, d], sq_recv.at[s, d],
                 {"head": lax.rem(head + d + 1, head_count)})
            for d in range(head_count - 1)
        ]
        for s in range(spans)
    ]

    def apply(s):
        pre_act = jnp.dot(queries[s], copy_in[...], preferred_element_type=jnp.float32)
        gate = pre_act[:, :hidden_units]
        hidden = (gate * jax.nn.sigmoid(gate) * pre_act[:, hidden_units:]).astype(jnp.bfloat16)
        made = contract_cols(hidden, copy_out[...])
        produced[s] = made
        sums = jnp.sum(made * made, axis=1, keepdims=True)
        squares[s, head] = jnp.transpose(jnp.broadcast_to(sums, (rows, 128)))[:8]
        for copy in square[s]:
            send(copy)

    def finish(s):
        for copy in square[s]:
            copy.wait_recv()
        total = squares[s, 0]
        for h in range(1, head_count):
            total = total + squares[s, h]
        scale = lax.rsqrt(total / (head_size * head_count) + out_eps)
        column = jnp.transpose(jnp.concatenate([scale] * 16, axis=0))[:, :1]
        res_ref[0, s] = (produced[s] * column * gain_ref[...]).astype(jnp.bfloat16)

    own_across(1, 1)
    start_own(0, 0)
    own_across(0, 1)
    own_weights(1)
    pass_x(1, 0, 1)
    pass_x(0, 0, 1)
    own_across(0, 0)
    pass_x(0, 0, 0)
    pass_x(1, 0, 0)
    own_across(1, 0)
    start_own(0, 1)
    pass_z(0, 2, 0)
    pass_weights(1, 1)
    pass_z(0, 1, 0)
    pass_z(0, 1, 1)
    own_weights(3)
    pass_weights(1, 3)
    for copy in loads[2:]:
        copy.wait()
    unpack(tok)
    project_queries(0)
    own_weights(2)
    pass_z(1, 2, 1)
    start_own(1, 0)
    pass_z(0, 2, 1)
    pass_weights(2, 1)
    pass_x(0, 1, 0)
    pass_x(0, 1, 1)
    pass_z(0, 3, 0)
    pass_x(0, 2, 0)
    pass_z(1, 1, 0)
    own_weights(0)
    pass_z(1, 2, 0)
    pass_weights(2, 3)
    pass_x(0, 2, 1)
    pass_z(1, 1, 1)
    pass_weights(3, 1)
    pass_z(0, 3, 1)
    pass_z(1, 3, 0)
    pass_weights(2, 2)
    pass_x(1, 2, 1)
    pass_x(0, 3, 0)
    pass_y(0, 1, 0)
    project_queries(1)
    pass_weights(3, 3)
    pass_x(0, 3, 1)
    pass_weights(2, 0)
    pass_weights(1, 2)
    pass_y(0, 0, 1)
    pass_y(0, 0, 0)
    pass_weights(1, 0)
    pass_weights(3, 0)
    pass_weights(3, 2)
    pass_y(1, 0, 1)
    pass_y(0, 2, 1)
    pass_x(1, 1, 0)
    take(0, 0)
    pass_y(0, 1, 1)
    pass_x(1, 2, 0)
    pass_z(1, 3, 1)
    pass_x(1, 3, 0)
    pass_y(1, 0, 0)
    pass_x(1, 1, 1)
    pass_y(0, 2, 0)
    pass_y(0, 3, 1)
    take(0, 1)
    pass_y(1, 2, 1)
    take(1, 0)
    pass_y(0, 3, 0)
    take(0, 2)
    unpack_all()
    pass_y(1, 1, 0)
    pass_y(1, 2, 0)
    take(0, 3)
    pass_y(1, 1, 1)
    pass_x(1, 3, 1)
    add_grads(0, 0, 4)
    update(0)
    start_own(1, 1)
    take(1, 1)
    take(1, 2)
    apply(0)
    pass_y(1, 3, 0)
    pass_y(1, 3, 1)
    add_grads(1, 0, 3)
    take(1, 3)
    add_grads(1, 3, 1)
    update(1)
    apply(1)
    finish(0)
    finish(1)
    for copy, cond in sent:
        if cond is None:
            copy.wait_send()
        else:
            pl.when(cond)(copy.wait_send)


def by_kernel(sizes, views, q_weight, k_weight, v_weight, rate_weight, fast_in, fast_out, out_gain):
    tok_count, grp_count, head_count = sizes
    _, spans, rows, width = views.shape
    _, head_size, block_in = fast_in.shape
    _, hidden_units, block_out = fast_out.shape
    piece = width // (grp_count * head_count)
    fold = hidden_units * block_out // head_size
    dma = pltpu.SemaphoreType.DMA
    vmem = pltpu.VMEM
    return pl.pallas_call(
        functools.partial(fused_kernel, tok_count, grp_count, head_count),
        out_shape=jax.ShapeDtypeStruct((1, spans, rows, head_size), jnp.bfloat16),
        in_specs=[pl.BlockSpec(memory_space=pl.ANY)] * 8,
        out_specs=pl.BlockSpec(memory_space=pltpu.VMEM),
        scratch_shapes=[
            vmem((spans, rows, width), jnp.bfloat16),
            *[vmem((width, head_size), jnp.bfloat16)] * 3,
            vmem((1, width), jnp.bfloat16),
            vmem((head_size, block_in), jnp.float32),
            vmem((block_out, hidden_units), jnp.float32),
            vmem((1, head_size), jnp.float32),
            vmem((spans, tok_count, head_count, grp_count, rows, piece), jnp.bfloat16),
            vmem((tok_count, head_size, block_in + fold), jnp.bfloat16),
            vmem((spans, rows, head_size), jnp.bfloat16),
            vmem((spans, tok_count * rows, head_size), jnp.bfloat16),
            vmem((spans, tok_count * rows, head_size), jnp.bfloat16),
            vmem((head_size, 2 * hidden_units), jnp.float32),
            vmem((head_size, hidden_units), jnp.float32),
            vmem((head_size, 2 * hidden_units), jnp.float32),
            vmem((head_size, hidden_units), jnp.float32),
            vmem((head_size, 2 * hidden_units), jnp.bfloat16),
            vmem((head_size, hidden_units), jnp.bfloat16),
            vmem((1, 2 * hidden_units), jnp.float32),
            vmem((head_size, 1), jnp.float32),
            vmem((spans, rows, head_size), jnp.float32),
            vmem((spans, head_count, 8, rows), jnp.float32),
            dma((8,)), dma((spans, head_count, grp_count)),
            dma((spans, tok_count, grp_count, 3)), dma((spans, tok_count, grp_count)),
            *[dma((spans, tok_count, grp_count))] * 8,
            dma((tok_count, 4, 3)), dma((tok_count, 4)),
            *[dma((tok_count, 4))] * 2,
            *[dma((spans, head_count - 1))] * 2,
        ],
        compiler_params=pltpu.CompilerParams(collective_id=0, has_side_effects=True),
        name="fused_layer",
    )(
        views, q_weight, k_weight, v_weight, rate_weight.T, fast_in,
        jnp.swapaxes(fast_out, 1, 2), out_gain.reshape(1, -1),
    )


def local(sizes, views, *rest):
    tok_count, grp_count, head_count = sizes
    fast_in, fast_out = rest[4], rest[5]
    head_size, hidden_units = fast_in.shape[1], fast_out.shape[1]
    piece = views.shape[3] // (grp_count * head_count)
    few = tok_count * views.shape[2] <= 4 * head_size
    fits = (
        tok_count == 4 and grp_count == 2 and head_count == 4 and piece % 128 == 0
        and fast_in.shape[2] % 128 == 0 and views.shape[2] % 16 == 0 and head_size % fast_out.shape[2] == 0
        and fast_out.shape[2] * hidden_units % (128 * head_size) == 0 and fast_out.shape[2] % 16 == 0
    )
    if few and fits:
        return by_kernel(sizes, views, *rest)
    return by_collectives(views, *rest)


def solution(mesh):
    sizes = (mesh.shape["tok"], mesh.shape["grp"], mesh.shape["head"])
    placed = (
        P("grp", None, "tok", None),
        P(None, "head"),
        P(None, "head"),
        P(None, "head"),
        P(None, "head"),
        P("head", None, "tok"),
        P("head", None, "tok"),
        P("head"),
    )
    return jax.shard_map(
        functools.partial(local, sizes), mesh=mesh, in_specs=placed, out_specs=P("grp", None, "tok", "head"), check_vma=False
    )
```
